256 devices in a mesh: ha: 8 (over z_lo, core), wa: 32 (over y, x, z_hi).
Axes of the slice: x: 4, y: 4, z: 8 (z_hi: 2, z_lo: 4; z = z_hi * 4 + z_lo), core: 2. Of those that a mesh axis runs over, the one named last changes fastest.
Arguments:
- tokens: bfloat16 [1, 8, 64, 64, 1152], P(None, None, 'ha', 'wa'), may hold values from -36 to 36
- cotangent: bfloat16 [1, 8, 64, 64, 1152], P(None, None, 'ha', 'wa'), may hold values from -6 to 6
- w_qkv: bfloat16 [3, 1152, 1728], P(None, 'wa'), may hold values from -0.1875 to 0.1875
- w_out: bfloat16 [3, 576, 1152], P(None, 'wa'), may hold values from -0.25 to 0.25
- gains: float32 [3, 1152], replicated, may hold values from 0.1 to 1.9
- gates: float32 [3, 8], replicated, may hold values from 0.5 to 2
Outputs:
- token_grad: bfloat16 [1, 8, 64, 64, 1152], P(None, None, 'ha', 'wa')
- head_sens: bfloat16 [1, 3, 8, 64, 64, 8], P(None, None, None, 'ha', 'wa')
The draws below stay inside these ranges and needn't reach their ends.
All inputs are finite; a program needn't handle non-finite values.
Results may differ from the reference program's by a relative error of at most 0.02.
Values may be sent and summed in bfloat16 or wider, within the bound.
A program may use at most 128 MiB of HBM per device.

```python
import math
import jax
import jax.numpy as jnp
from jax import lax

D = 1152
HEADS = 8
F = 8
B = 1
H = 64
W = 64
HD = 576


def draw_tokens(key, part):
    pieces = jax.random.split(jax.random.fold_in(key, 11), 3)
    full_shape = (B, F, H, W, D)
    row_scale = jnp.exp(jax.random.uniform(pieces[0], (B, F, H, W, 1), minval=math.log(0.3), maxval=math.log(3.0)))
    column_scale = jnp.exp(jax.random.uniform(pieces[1], (D,), minval=math.log(0.3), maxval=math.log(3.0)))
    base_draw = jnp.clip(jax.random.normal(pieces[2], full_shape), -4.0, 4.0)
    return (base_draw * row_scale * column_scale).astype(jnp.bfloat16)


def shard_levels(own_key, dims, cuts, low, top_value):
    level, own = 1.0, jax.random.fold_in(own_key, 6)
    for dim, shards_of in cuts:
        steps = jnp.exp(jax.random.uniform(jax.random.fold_in(own, dim), (shards_of,), jnp.float32, low / len(cuts), top_value / len(cuts)))
        level = level * jnp.repeat(steps, dims[dim] // shards_of).reshape([-1 if axis == dim else 1 for axis in range(len(dims))])
    return level


def noise(own_key, shape, width, reach, cuts=(), dtype=jnp.bfloat16):
    drawn = jax.random.normal(own_key, shape, jnp.float32) * width
    if len(cuts) > 0:
        drawn = shard_levels(own_key, shape, cuts, -0.22, 0.18) * drawn
    return jnp.clip(drawn, min=-reach, max=reach).astype(dtype)


def setup_inputs(seed: int = 0) -> dict:
    keys = jax.random.split(jax.random.key(seed), 7)
    tokens = draw_tokens(jax.random.fold_in(keys[6], 71), 0)
    cotangent = noise(keys[1], (B, F, H, W, D), 1.0, 6.0, ((2, 8), (3, 32)))
    w_qkv = noise(keys[2], (3, D, 3 * HD), D ** -0.5, 0.1875, ((1, 32),))
    w_out = noise(keys[3], (3, HD, D), HD ** -0.5, 0.25, ((1, 32),))
    gains = jnp.clip(1.0 + 0.18 * jax.random.normal(keys[4], (3, D), jnp.float32), 0.1, 1.9)
    gates = jnp.clip(jnp.exp(jax.random.uniform(keys[5], (3, HEADS), jnp.float32, math.log(0.5), math.log(2.0))), 0.5, 2.0)
    return dict(tokens=tokens, cotangent=cotangent, w_qkv=w_qkv, w_out=w_out, gains=gains, gates=gates)


def letter_forms(attend_axis):
    letters = 'bfhw'
    query_side = letters + 'nc'
    key_side = letters[:attend_axis] + 'g' + letters[attend_axis + 1:] + 'nc'
    score_side = letters[:attend_axis] + letters[attend_axis + 1:] + 'n' + letters[attend_axis] + 'g'
    return (query_side + ',' + key_side + '->' + score_side, score_side + ',' + key_side + '->' + query_side, score_side + ',' + query_side + '->' + key_side)

def product(form, left, right):
    return jnp.einsum(form, left.astype(jnp.float32), right.astype(jnp.float32))

def forward_sublayer(inputs, w_qkv, w_out, gain, gate, attend_axis):
    scores_form, mixing_form, keyward_form = letter_forms(attend_axis)
    heads = gate.shape[0]
    hidden = w_out.shape[0]
    head_dim = hidden // heads
    leading = inputs.shape[:4]
    inputs_f = inputs.astype(jnp.float32)
    inverse = lax.rsqrt(lax.optimization_barrier(jnp.mean(inputs_f * inputs_f, axis=-1, keepdims=True)) + 1e-06)
    normed = (inputs_f * inverse * gain).astype(jnp.bfloat16)
    projected = jnp.dot(normed, w_qkv, preferred_element_type=jnp.float32).astype(jnp.bfloat16)
    split = projected.reshape(leading + (3, heads, head_dim))
    queries = split[..., 0, :, :]
    keys_all = split[..., 1, :, :]
    values = split[..., 2, :, :]
    scores = product(scores_form, queries, keys_all) * head_dim ** (-0.5)
    raised = jnp.exp(scores)
    probs = raised / lax.optimization_barrier(jnp.sum(raised, axis=-1, keepdims=True))
    probs_half = probs.astype(jnp.bfloat16)
    attended = product(mixing_form, probs_half, values).astype(jnp.bfloat16)
    gated = (attended.astype(jnp.float32) * gate[:, None]).astype(jnp.bfloat16).reshape(leading + (hidden,))
    outputs = (inputs_f + jnp.dot(gated, w_out, preferred_element_type=jnp.float32)).astype(jnp.bfloat16)
    return (outputs, (inverse, queries, keys_all, values, probs, probs_half, attended))

def backward_sublayer(outgrad, inputs, saved, w_qkv, w_out, gain, gate, attend_axis):
    scores_form, mixing_form, keyward_form = letter_forms(attend_axis)
    inverse, queries, keys_all, values, probs, probs_half, attended = saved
    heads = gate.shape[0]
    hidden = w_out.shape[0]
    head_dim = hidden // heads
    leading = inputs.shape[:4]
    d_gated = jnp.dot(outgrad, w_out.T, preferred_element_type=jnp.float32).astype(jnp.bfloat16)
    d_gated = d_gated.reshape(leading + (heads, head_dim))
    sens = lax.optimization_barrier(jnp.sum(d_gated.astype(jnp.float32) * attended.astype(jnp.float32), axis=-1)).astype(jnp.bfloat16)
    d_attended = (d_gated.astype(jnp.float32) * gate[:, None]).astype(jnp.bfloat16)
    d_probs = product(scores_form, d_attended, values)
    d_values = product(keyward_form, probs_half, d_attended)
    d_scores = (probs * (d_probs - lax.optimization_barrier(jnp.sum(d_probs * probs, axis=-1, keepdims=True))) * head_dim ** (-0.5)).astype(jnp.bfloat16)
    d_queries = product(mixing_form, d_scores, keys_all)
    d_keys = product(keyward_form, d_scores, queries)
    d_proj = jnp.stack([d_queries, d_keys, d_values], axis=4).reshape(leading + (3 * hidden,)).astype(jnp.bfloat16)
    d_normed = jnp.dot(d_proj, w_qkv.T, preferred_element_type=jnp.float32) * gain
    inputs_f = inputs.astype(jnp.float32)
    ingrad = outgrad.astype(jnp.float32) + inverse * d_normed - inputs_f * inverse * inverse * inverse * lax.optimization_barrier(jnp.mean(inputs_f * d_normed, axis=-1, keepdims=True))
    return (ingrad.astype(jnp.bfloat16), sens)

def reference(tokens, cotangent, w_qkv, w_out, gains, gates):

    def one_video(pair):
        video = pair[0][None]
        video_cot = pair[1][None]
        after_time, saved_time = forward_sublayer(video, w_qkv[0], w_out[0], gains[0], gates[0], 1)
        after_height, saved_height = forward_sublayer(after_time, w_qkv[1], w_out[1], gains[1], gates[1], 2)
        unused_out, saved_width = forward_sublayer(after_height, w_qkv[2], w_out[2], gains[2], gates[2], 3)
        grad_width, sens_width = backward_sublayer(video_cot, after_height, saved_width, w_qkv[2], w_out[2], gains[2], gates[2], 3)
        grad_height, sens_height = backward_sublayer(grad_width, after_time, saved_height, w_qkv[1], w_out[1], gains[1], gates[1], 2)
        grad_time, sens_time = backward_sublayer(grad_height, video, saved_time, w_qkv[0], w_out[0], gains[0], gates[0], 1)
        return (grad_time[0], jnp.stack([sens_time[0], sens_height[0], sens_width[0]], axis=0))
    token_grad, head_sens = lax.map(one_video, (tokens, cotangent))
    return (token_grad, head_sens)
```

```python
import functools
import jax
import jax.numpy as jnp
from jax import lax
from jax.experimental import pallas as pl
from jax.experimental.pallas import tpu as pltpu
from jax.sharding import PartitionSpec as P

MESH = pl.DeviceIdType.MESH
QR, QC, OR, OC = 72, 896, 40, 640
BF = jnp.bfloat16
F32 = jnp.float32


def place():
    ha = lax.axis_index("ha")
    wa = lax.axis_index("wa")
    return ha // 2, ha % 2, wa // 8, (wa // 2) % 4, wa % 2


def gather_kernel(sq, so, gq, go, rq, ro, dq, do, lsem, zs, zr, ssem, rsem):
    zl, c, y, x, zh = place()
    ha = zl * 2 + c

    def dev(yy, xx):
        return (ha, (yy * 4 + xx) * 2 + zh)

    def along(d1, d2):
        dy = jnp.where(c == 0, d2, d1)
        dx = jnp.where(c == 0, d1, d2)
        return (y + dy + 4) % 4, (x + dx + 4) % 4

    def slot(d1, d2):
        yy, xx = along(d1, d2)
        return yy * 4 + xx

    ends = (zl == 0) | (zl == 3)
    near = 3 - zl
    far = jnp.where(zl == 3, 1, 2)
    zdev1 = (near * 2 + c, (y * 4 + x) * 2 + 1 - zh)
    zdev2 = (far * 2 + c, (y * 4 + x) * 2 + 1 - zh)
    zsrc_l = jnp.where(zl >= 2, 0, 3)
    zsrc = (zsrc_l * 2 + c, (y * 4 + x) * 2 + 1 - zh)
    sib = (zl * 2 + 1 - c, (y * 4 + x) * 2 + zh)
    p1 = {d: dev(*along(d, 0)) for d in (1, -1)}
    p2 = {d: dev(*along(0, d)) for d in (1, -1)}

    barrier = pltpu.get_barrier_semaphore()
    for t in (sib, p1[1], p1[-1], p2[1], p2[-1], zsrc):
        pl.semaphore_signal(barrier, inc=1, device_id=t, device_id_type=MESH)

    @pl.when(ends)
    def _():
        for t in (zdev1, zdev2):
            pl.semaphore_signal(barrier, inc=1, device_id=t, device_id_type=MESH)

    lq = pltpu.make_async_copy(sq.at[c], rq.at[zh], lsem.at[0])
    lo = pltpu.make_async_copy(so.at[c], ro.at[zh], lsem.at[1])
    lq.start()
    lo.start()
    pl.semaphore_wait(barrier, 6 + 2 * jnp.where(ends, 1, 0))

    def zcopy(src, dst, i, k, t):
        return pltpu.make_async_remote_copy(
            src_ref=src, dst_ref=dst, send_sem=zs.at[i, k], recv_sem=zr.at[k],
            device_id=t, device_id_type=MESH)

    @pl.when(ends)
    def _():
        for i, t in enumerate((zdev1, zdev2)):
            zcopy(sq.at[c], rq.at[zh], i, 0, t).start()
            zcopy(so.at[c], ro.at[zh], i, 1, t).start()

    lq.wait()
    lo.wait()
    zcopy(sq.at[c], rq.at[1 - zh], 0, 0, zdev1).wait_recv()
    zcopy(so.at[c], ro.at[1 - zh], 0, 1, zdev1).wait_recv()

    def perm(n, half, pad):
        r = lax.broadcasted_iota(jnp.int32, (n, 2 * pad), 0)
        k = lax.broadcasted_iota(jnp.int32, (n, 2 * pad), 1)
        want = jnp.where(r < half, r, jnp.where(r < 2 * half, r + pad - half, -1))
        return (k == want).astype(F32).astype(BF)

    pq = perm(QR, 36, 48)
    po = perm(OR, 18, 32)
    for l in range(3):
        dq[l] = jnp.dot(pq, rq[:, l].reshape(96, QC), preferred_element_type=F32).astype(BF)
        do[l] = jnp.dot(po, ro[:, l].reshape(64, OC), preferred_element_type=F32).astype(BF)

    sends = []
    n_send = [0]

    QP = ((0, 40), (40, 32))
    OP = ((0, 16), (16, 24))

    def qrows(half, s, part):
        o, n = (0, QR) if part is None else QP[part]
        return gq.at[half, :, pl.ds(pl.multiple_of(s * QR + o, 8), n), :]

    def orows(half, s, part):
        o, n = (0, OR) if part is None else OP[part]
        return go.at[half, :, pl.ds(pl.multiple_of(s * OR + o, 8), n), :]

    def send(s, part, r, t, own=False, half=None):
        half = c if half is None else half
        for k, (rows, d) in enumerate(((qrows, dq), (orows, do))):
            cp = pltpu.make_async_remote_copy(
                src_ref=d if own else rows(half, s, part), dst_ref=rows(half, s, part),
                send_sem=ssem.at[n_send[0], k], recv_sem=rsem.at[r, k],
                device_id=t, device_id_type=MESH)
            cp.start()
            sends.append(cp)
        n_send[0] += 1

    def recv(s, part, r, half=None):
        half = c if half is None else half
        for k, rows in enumerate((qrows, orows)):
            pltpu.make_async_remote_copy(
                src_ref=rows(half, s, part), dst_ref=rows(half, s, part),
                send_sem=ssem.at[0, k], recv_sem=rsem.at[r, k],
                device_id=sib, device_id_type=MESH).wait_recv()

    def m2(b, k):
        return 4 + 4 * b + k

    own = slot(0, 0)
    lq2 = pltpu.make_async_copy(dq, qrows(c, own, None), lsem.at[0])
    lo2 = pltpu.make_async_copy(do, orows(c, own, None), lsem.at[1])
    D1 = (0, -1, 1, 2)

    def sibling(i, j, s, own=False):
        send(s, None, 20 + 4 * i + j, sib, own=own)

    send(own, None, 0, p1[1], own=True)
    send(own, None, 1, p1[-1], own=True)
    send(own, None, m2(0, 0), p2[1], own=True)
    send(own, None, m2(0, 1), p2[-1], own=True)
    lq2.start()
    lo2.start()
    sibling(0, 0, own, own=True)
    for b, d in ((1, -1), (2, 1)):
        s = slot(d, 0)
        recv(s, None, b - 1)
        send(s, b - 1, 2 + (b - 1), p1[-d])
        send(s, None, m2(b, 0), p2[1])
        send(s, None, m2(b, 1), p2[-1])
        sibling(b, 0, s)
    s = slot(2, 0)
    recv(s, 0, 2)
    recv(s, 1, 3)
    send(s, None, m2(3, 0), p2[1])
    send(s, None, m2(3, 1), p2[-1])
    sibling(3, 0, s)
    for b, d in enumerate(D1):
        for k, e in ((0, -1), (1, 1)):
            s = slot(d, e)
            recv(s, None, m2(b, k))
            send(s, k, m2(b, 2 + k), p2[-e])
            sibling(b, 1 + k, s)
    for b, d in enumerate(D1):
        s = slot(d, 2)
        recv(s, 0, m2(b, 2))
        recv(s, 1, m2(b, 3))
        sibling(b, 3, s)
    lq2.wait()
    lo2.wait()
    for i, d in enumerate(D1):
        for j, e in enumerate((0, -1, 1, 2)):
            recv(slot(e, d), None, 20 + 4 * i + j, half=1 - c)
    for cp in sends:
        cp.wait_send()

    @pl.when(ends)
    def _():
        for i, t in enumerate((zdev1, zdev2)):
            zcopy(sq.at[c], rq.at[zh], i, 0, t).wait_send()
            zcopy(so.at[c], ro.at[zh], i, 1, t).wait_send()


def gather(sq, so):
    return pl.pallas_call(
        gather_kernel,
        out_shape=(jax.ShapeDtypeStruct((2, 3, 1152, QC), BF), jax.ShapeDtypeStruct((2, 3, 640, OC), BF)),
        in_specs=[pl.BlockSpec(memory_space=pl.ANY)] * 2,
        out_specs=(pl.BlockSpec(memory_space=pl.ANY),) * 2,
        scratch_shapes=[
            pltpu.VMEM((2, 3, 48, QC), BF), pltpu.VMEM((2, 3, 32, OC), BF),
            pltpu.VMEM((3, QR, QC), BF), pltpu.VMEM((3, OR, OC), BF),
            pltpu.SemaphoreType.DMA((2,)),
            pltpu.SemaphoreType.DMA((2, 2)), pltpu.SemaphoreType.DMA((2,)),
            pltpu.SemaphoreType.DMA((36, 2)), pltpu.SemaphoreType.DMA((36, 2)),
        ],
        compiler_params=pltpu.CompilerParams(collective_id=0, has_side_effects=True),
        name="weights",
    )(sq, so)


def shard_halves(w_qkv, w_out):
    v = jnp.pad(w_qkv[..., 1152:].reshape(3, 36, 16, 36), ((0, 0), (0, 0), (0, 0), (0, 4))).reshape(3, 36, 640)
    q = jnp.concatenate([w_qkv[..., :1152], v], axis=-1)
    q = jnp.pad(q, ((0, 0), (0, 12), (0, 0)))
    o = jnp.pad(w_out, ((0, 0), (0, 14), (0, 128)))
    return (jnp.stack([q[..., :896], q[..., 896:]]), jnp.stack([o[..., :640], o[..., 640:]]))


SCALE = 72 ** (-0.5)
HEADS = 8


def dot(a, b):
    return jnp.dot(a, b, preferred_element_type=F32)


def dot_nt(a, b):
    return lax.dot_general(a, b, (((1,), (1,)), ((), ())), preferred_element_type=F32)


def dot_tn(a, b):
    return lax.dot_general(a, b, (((0,), (0,)), ((), ())), preferred_element_type=F32)


def window(h, width):
    lo = (width * h) // 128 * 128
    hi = -(-(width * (h + 1)) // 128) * 128
    return lo, hi


def lanes(h, width):
    lo, hi = window(h, width)
    i = lax.broadcasted_iota(jnp.int32, (1, hi - lo), 1) + lo
    return ((i >= width * h) & (i < width * (h + 1))).astype(F32).astype(BF)


class Tiles:
    def __init__(self):
        self.t = [None] * 5

    def add(self, lo, value):
        for n in range(value.shape[1] // 128):
            part = value[:, 128 * n:128 * (n + 1)]
            at = lo // 128 + n
            self.t[at] = part if self.t[at] is None else self.t[at] + part

    def all(self):
        return jnp.concatenate(self.t, axis=1)


def same_line(layer):
    r = lax.broadcasted_iota(jnp.int32, (128, 128), 0)
    k = lax.broadcasted_iota(jnp.int32, (128, 128), 1)
    if layer == 0:
        return (r % 16) == (k % 16)
    if layer == 1:
        return (r % 2) == (k % 2)
    return ((r // 2) % 2) == ((k // 2) % 2)


def spread(second):
    r = lax.broadcasted_iota(jnp.int32, (256, 128), 0)
    k = lax.broadcasted_iota(jnp.int32, (256, 128), 1)
    r8 = r % 8
    want = (r // 8) * 4 + r8 - (4 if second else 0)
    ok = (r8 >= 4) if second else (r8 < 4)
    return ((k == want) & ok).astype(F32).astype(BF)


def collect(second):
    r = lax.broadcasted_iota(jnp.int32, (128, 256), 0)
    k = lax.broadcasted_iota(jnp.int32, (128, 256), 1)
    return (k == (r // 4) * 8 + r % 4 + (4 if second else 0)).astype(F32).astype(BF)


def pack(ref, x, y):
    s = dot(spread(False), x) + dot(spread(True), y)
    ref[...] = s.reshape(32, 8, 640).astype(BF)


def unpack(ref):
    r = ref[...].astype(F32).reshape(256, 640).astype(BF)
    a = dot(collect(False), r)
    b = dot(collect(True), r)
    return jnp.concatenate([a, b[:, 128:]], axis=1).astype(BF), b[:, :128].astype(BF)


class Net:
    def __init__(self, ssem, rsem):
        self.ha = lax.axis_index("ha")
        self.wa = lax.axis_index("wa")
        self.ssem, self.rsem = ssem, rsem

    def barrier(self):
        b = pltpu.get_barrier_semaphore()

        def ha(k, u):
            pl.semaphore_signal(b, inc=1, device_id=((self.ha + k) % 8, self.wa), device_id_type=MESH)
            return u

        def wa(k, u):
            pl.semaphore_signal(b, inc=1, device_id=(self.ha, (self.wa + k) % 32), device_id_type=MESH)
            return u

        lax.fori_loop(1, 8, ha, 0)
        lax.fori_loop(1, 32, wa, 0)
        pl.semaphore_wait(b, 38)

    def send_ha(self, n, src, dst):
        me = pl.ds(pl.multiple_of(self.ha * 16, 16), 16)

        def one(k, u):
            j = (self.ha + k) % 8
            pltpu.make_async_remote_copy(
                src_ref=src.at[pl.ds(pl.multiple_of(j * 16, 16), 16)], dst_ref=dst.at[me],
                send_sem=self.ssem.at[n], recv_sem=self.rsem.at[n],
                device_id=(j, self.wa), device_id_type=MESH).start()
            return u

        lax.fori_loop(1, 8, one, 0)
        dst[me] = src[me]

    def send_wa(self, n, src, dst):
        def one(k, u):
            j = (self.wa + k) % 32
            pltpu.make_async_remote_copy(
                src_ref=src.at[j], dst_ref=dst.at[self.wa],
                send_sem=self.ssem.at[n], recv_sem=self.rsem.at[n],
                device_id=(self.ha, j), device_id_type=MESH).start()
            return u

        lax.fori_loop(1, 32, one, 0)
        dst[self.wa] = src[self.wa]

    def wait(self, sems, n, ref):
        part = ref.at[pl.ds(0, 112)] if ref.shape[0] == 128 else ref.at[pl.ds(0, 31)]
        pltpu.make_async_copy(part, part, sems.at[n]).wait()


def step_kernel(x0, cot, gq, go, gains, gates, grad, sens,
                wq, wo, q_s, k_s, v_s, a_s, p_s, x1s, x1, c1, cs, cr, x2s, x2r, g2s, g2r, g1s, g1r,
                wsem, ssem, rsem):
    net = Net(ssem, rsem)
    loads = []
    for l in range(3):
        cps = [pltpu.make_async_copy(gq.at[c, l], wq.at[c, l], wsem.at[l, c]) for c in range(2)]
        cps += [pltpu.make_async_copy(go.at[c, l], wo.at[c, l], wsem.at[l, 2 + c]) for c in range(2)]
        for cp in cps:
            cp.start()
        loads.append(cps)
    net.barrier()
    net.send_ha(0, cot, c1)

    def norm(x):
        xf = x.astype(F32)
        return xf, lax.rsqrt(jnp.mean(xf * xf, axis=-1, keepdims=True) + 1e-06)

    def forward(l, x):
        gain = gains[l:l + 1, :]
        xf, inv = norm(x)
        normed = (xf * inv * gain).astype(BF)
        a = dot(normed, wq[0, l])
        b = dot(normed, wq[1, l])
        q_s[l] = a[:, :640].astype(BF)
        k_s[l] = pltpu.roll(jnp.concatenate([a[:, 512:], b[:, :256]], axis=1), 576, 1).astype(BF)
        v_s[l] = b[:, 256:].astype(BF)
        line = same_line(l)
        att = Tiles()
        for h in range(HEADS):
            lo, hi = window(h, 72)
            s = dot_nt(q_s[l, :, lo:hi] * lanes(h, 72), k_s[l, :, lo:hi]) * SCALE
            e = jnp.where(line, jnp.exp(s), 0.0)
            p = e / jnp.sum(e, axis=-1, keepdims=True)
            p_s[l, h] = p
            lo, hi = window(h, 80)
            att.add(lo, dot(p.astype(BF), v_s[l, :, lo:hi] * lanes(h, 80)))
        a_s[l] = att.all().astype(BF)

    def output(l, x):
        gated = (a_s[l].astype(F32) * gates[l:l + 1, :]).astype(BF)
        o = jnp.concatenate([dot(gated, wo[0, l]), dot(gated, wo[1, l, :, :512])], axis=1)
        return (x.astype(F32) + o).astype(BF)

    def dgated_of(l, og):
        return (dot_nt(og[:, :640], wo[0, l]) + dot_nt(og[:, 640:], wo[1, l, :, :512])).astype(BF)

    def backward(l, og, x, dg):
        gain = gains[l:l + 1, :]
        prod = dg.astype(F32) * a_s[l].astype(F32)
        high = prod.astype(BF)
        low = (prod - high.astype(F32)).astype(BF)
        i = lax.broadcasted_iota(jnp.int32, (640, 128), 0)
        k = lax.broadcasted_iota(jnp.int32, (640, 128), 1)
        pick = ((i >= 80 * (k - 8 * l)) & (i < 80 * (k - 8 * l) + 80)).astype(F32).astype(BF)
        sn = dot(high, pick) + dot(low, pick)
        da = (dg.astype(F32) * gates[l:l + 1, :]).astype(BF)
        dq, dk, dv = Tiles(), Tiles(), Tiles()
        for h in range(HEADS):
            lo, hi = window(h, 80)
            p = p_s[l, h]
            dah = da[:, lo:hi] * lanes(h, 80)
            dp = dot_nt(dah, v_s[l, :, lo:hi])
            dv.add(lo, dot_tn(p.astype(BF), dah))
            ds = (p * (dp - jnp.sum(dp * p, axis=-1, keepdims=True)) * SCALE).astype(BF)
            lo, hi = window(h, 72)
            m = lanes(h, 72)
            dq.add(lo, dot(ds, k_s[l, :, lo:hi] * m))
            dk.add(lo, dot_tn(ds, q_s[l, :, lo:hi] * m))
        dqv = dq.all()
        dkv = pltpu.roll(dk.all(), 64, 1)
        dqk = jnp.concatenate([dqv[:, :512], dqv[:, 512:] + dkv[:, :128], dkv[:, 128:]], axis=1)
        d0 = dqk[:, :896].astype(BF)
        d1 = jnp.concatenate([dqk[:, 896:], dv.all()], axis=1).astype(BF)
        dn = (dot_nt(d0, wq[0, l]) + dot_nt(d1, wq[1, l])) * gain
        xf, inv = norm(x)
        g = og.astype(F32) + inv * dn - xf * inv * inv * inv * jnp.mean(xf * dn, axis=-1, keepdims=True)
        return g.astype(BF), sn

    for cp in loads[0]:
        cp.wait()
    forward(0, x0[...])
    x1s[...] = output(0, x0[...])
    net.send_ha(1, x1s, x1)

    net.wait(rsem, 0, c1)
    pack(cs, c1[:, :640], c1[:, 512:])
    net.send_wa(2, cs, cr)
    for cp in loads[1]:
        cp.wait()
    net.wait(rsem, 1, x1)
    forward(1, x1[...])
    o1 = output(1, x1[...])
    pack(x2s, o1[:, :640], o1[:, 512:])
    net.send_wa(3, x2s, x2r)
    for cp in loads[2]:
        cp.wait()
    net.wait(rsem, 2, cr)
    og2, _ = unpack(cr)
    dg2 = dgated_of(2, og2)
    net.wait(rsem, 3, x2r)
    xx2, _ = unpack(x2r)
    forward(2, xx2)
    g2, sn2 = backward(2, og2, xx2, dg2)
    pack(g2s, g2[:, :640], jnp.concatenate([sn2.astype(BF), g2[:, 640:]], axis=1))
    net.send_wa(4, g2s, g2r)
    net.wait(rsem, 4, g2r)
    og1, sn2h = unpack(g2r)
    g1, sn1 = backward(1, og1, x1[...], dgated_of(1, og1))
    g1s[:, :1152] = g1
    g1s[:, 1152:] = (sn1 + sn2h.astype(F32)).astype(BF)
    net.send_ha(5, g1s, g1r)
    net.wait(rsem, 5, g1r)
    og0 = g1r[:, :1152]
    g0, sn0 = backward(0, og0, x0[...], dgated_of(0, og0))
    grad[...] = g0
    sens[...] = (sn0 + g1r[:, 1152:].astype(F32)).astype(BF)
    for n, ref in ((0, c1), (1, x1), (2, cr), (3, x2r), (4, g2r), (5, g1r)):
        net.wait(ssem, n, ref)


def steps(x, cot, gq, go, gains, gates):
    vm = pl.BlockSpec(memory_space=pltpu.VMEM)
    hb = pl.BlockSpec(memory_space=pl.ANY)
    tok = lambda n: pltpu.VMEM((128, n), BF)
    slots = pltpu.VMEM((32, 8, 640), BF)
    per = lambda: pltpu.VMEM((3, 128, 640), BF)
    return pl.pallas_call(
        step_kernel,
        out_shape=(jax.ShapeDtypeStruct((128, 1152), BF), jax.ShapeDtypeStruct((128, 128), BF)),
        in_specs=[vm, vm, hb, hb, vm, vm],
        out_specs=(vm, vm),
        scratch_shapes=[
            pltpu.VMEM((2, 3, 1152, 896), BF), pltpu.VMEM((2, 3, 640, 640), BF),
            per(), per(), per(), per(), pltpu.VMEM((3, HEADS, 128, 128), F32),
            tok(1152), tok(1152), tok(1152), slots, slots, slots, slots, slots, slots, tok(1280), tok(1280),
            pltpu.SemaphoreType.DMA((3, 4)), pltpu.SemaphoreType.DMA((6,)), pltpu.SemaphoreType.DMA((6,)),
        ],
        compiler_params=pltpu.CompilerParams(collective_id=1, has_side_effects=True, vmem_limit_bytes=60 << 20),
        name="steps",
    )(x, cot, gq, go, gains, gates)


def per_device(tokens, cotangent, w_qkv, w_out, gains, gates):
    gq, go = gather(*shard_halves(w_qkv, w_out))
    wide = jnp.repeat(gates, 80, axis=1)
    grad, sens = steps(tokens.reshape(128, 1152), cotangent.reshape(128, 1152), gq, go, gains, wide)
    head_sens = sens[:, :24].reshape(8, 8, 2, 3, 8).transpose(3, 0, 1, 2, 4)[None]
    return (grad.reshape(tokens.shape), head_sens)


def solution(mesh):
    in_specs = (
        P(None, None, "ha", "wa", None),
        P(None, None, "ha", "wa", None),
        P(None, "wa", None),
        P(None, "wa", None),
        P(),
        P(),
    )
    out_specs = (P(None, None, "ha", "wa", None), P(None, None, None, "ha", "wa", None))
    return jax.shard_map(
        per_device, mesh=mesh, in_specs=in_specs, out_specs=out_specs, check_vma=False
    )
```
